32 devices in a mesh: row: 16 (over z, y, x), col: 2 (over core).
Axes of the slice: x: 2, y: 2, z: 4, core: 2. Of those that a mesh axis runs over, the one named last changes fastest.
Arguments:
- integrals: bfloat16 [8192, 8192], P('row', 'col'), may hold values from -6 to 6
- amplitudes: bfloat16 [8192, 8192], P('row', 'col'), may hold values from -0.09375 to 0.09375
- pair_irrep: int32 [64], replicated, may hold values from 0 to 3
- tile_map: int32 [64], replicated, may hold values from 0 to 63, each once
Outputs:
- particle_hole: bfloat16 [8192, 8192], P('row', 'col')
The draws below stay inside these ranges and needn't reach their ends.
Inputs may be any that keep to these rules, and one draw needn't show every extreme that they name: `tile_map`: each of the 64 labelled tiles appears once.
All inputs are finite; a program needn't handle non-finite values.
Results may differ from the reference program's by a relative error of at most 0.0034.
Values may be sent and summed in bfloat16 or wider, within the bound.
No kernel may reach another device: no remote copies, remote signals or barrier semaphores. Data moves between devices by JAX's collectives and lax.ppermute only.
A program may use at most 128 MiB of HBM per device.

```python
import math
import jax
import jax.numpy as jnp
import numpy as np
from jax import lax

TILE = 128
NIRREP = 4
PAIR_TILES = 64
NPAIR = 8192


def with_ends(drawn, own_key, low, high):
    extent = drawn.shape
    spot = [jax.random.randint(jax.random.fold_in(own_key, axis), (), 0, extent[axis]) for axis in range(len(extent))]
    drawn = drawn.at[tuple(spot)].set(low)
    longest = extent.index(max(extent))
    spot[longest] = (spot[longest] + 1) % extent[longest]
    return drawn.at[tuple(spot)].set(high)


def level_of(stream_key, extent, split, smallest, high):
    def one(axis_at, shards_of):
        heights = jax.random.uniform(jax.random.fold_in(jax.random.fold_in(stream_key, 6), axis_at), (shards_of,), jnp.float32, smallest / len(split), high / len(split))
        return jnp.repeat(jnp.exp(heights), extent[axis_at] // shards_of).reshape((-1,) + (1,) * (len(extent) - axis_at - 1))

    loudness = one(*split[0])
    for cut in split[1:]:
        loudness = loudness * one(*cut)
    return loudness


def rank_bounds(amount, skew):
    loads = [(1 << 20) // math.isqrt(standing ** skew) + 1 for standing in range(1, amount + 1)]
    deviation = 1 + sum(loads) // (1 << 30)
    return np.cumsum(np.array([max(1, weight // deviation) for weight in loads]))


def skewed_ids(stream_key, extent, amount, lean):
    grid = rank_bounds(amount, lean)
    lot = jax.random.randint(jax.random.fold_in(stream_key, 1), extent, 0, int(grid[amount - 1]))
    standing = jnp.searchsorted(jnp.asarray(grid, jnp.int32), lot, side="right")
    return jax.random.permutation(jax.random.fold_in(stream_key, 2), amount)[standing].astype(jnp.int32)


def noise(own_key, shape, deviation, limit, pieces=(), kind=jnp.bfloat16):
    entries = jax.random.normal(own_key, shape, jnp.float32) * deviation
    if len(pieces) > 0:
        entries = level_of(own_key, shape, pieces, -0.22, 0.18) * entries
    return jnp.clip(entries, min=-limit, max=limit).astype(kind)


def setup_inputs(seed: int = 0) -> dict:
    keys = jax.random.split(jax.random.key(seed), 5)
    integrals = noise(keys[0], (NPAIR, NPAIR), 1.0, 6.0, ((0, 16), (1, 2)))
    amplitudes = noise(keys[1], (NPAIR, NPAIR), (NPAIR // 2) ** -0.5, 0.09375, ((0, 16), (1, 2)))
    pair_irrep = with_ends(skewed_ids(keys[2], (PAIR_TILES,), NIRREP, 2), jax.random.fold_in(keys[2], 3), 0, NIRREP - 1).astype(jnp.int32)
    tile_map = jax.random.permutation(keys[3], PAIR_TILES).astype(jnp.int32)
    return dict(integrals=integrals, amplitudes=amplitudes, pair_irrep=pair_irrep, tile_map=tile_map)


def reference(integrals, amplitudes, pair_irrep, tile_map):
    tile_irrep = pair_irrep[tile_map]
    labels = jnp.repeat(tile_irrep, TILE)
    masked_cols = jnp.where(labels[:, None] == labels[None, :], amplitudes, jnp.zeros((), amplitudes.dtype))
    block_rows = 1024

    def one_block(block_pair):
        rows_part, labels_part = block_pair
        masked_rows = jnp.where(labels_part[:, None] == labels[None, :], rows_part, jnp.zeros((), rows_part.dtype))
        return jnp.dot(masked_rows, masked_cols, preferred_element_type=jnp.float32).astype(jnp.bfloat16)

    blocks = lax.map(one_block, (integrals.reshape(NPAIR // block_rows, block_rows, NPAIR), labels.reshape(NPAIR // block_rows, block_rows)))
    return blocks.reshape(NPAIR, NPAIR)
```

```python
import functools

import jax
import jax.numpy as jnp
from jax import lax
from jax.experimental import pallas as pl
from jax.experimental.pallas import tpu as pltpu
from jax.sharding import PartitionSpec as P

TILE = 128
NIRREP = 4
Q = 4
GRP = 4

CLASSES = ((84, 20, 64),)


def tile_labels(pair_irrep, tile_map):
    labels = jnp.arange(pair_irrep.shape[0], dtype=jnp.int32)
    hits = tile_map[:, None] == labels[None, :]
    return jnp.sum(jnp.where(hits, pair_irrep[None, :], 0), axis=1)


def dense(integrals, amplitudes, pair_irrep, tile_map):
    row_index = lax.axis_index("row")
    col_index = lax.axis_index("col")
    row_width = integrals.shape[0]
    col_width = amplitudes.shape[1]
    index_labels = jnp.repeat(tile_labels(pair_irrep, tile_map), TILE)
    row_labels = lax.dynamic_slice_in_dim(index_labels, row_index * row_width, row_width)
    col_labels = lax.dynamic_slice_in_dim(index_labels, col_index * col_width, col_width)
    whole_rows = lax.all_gather(integrals, "col", axis=1, tiled=True)
    masked_rows = jnp.where(
        row_labels[:, None] == index_labels[None, :], whole_rows, jnp.zeros((), whole_rows.dtype)
    )
    whole_cols = lax.all_gather(amplitudes, "row", axis=0, tiled=True)
    masked_cols = jnp.where(
        index_labels[:, None] == col_labels[None, :], whole_cols, jnp.zeros((), whole_cols.dtype)
    )
    return jnp.dot(masked_rows, masked_cols, preferred_element_type=jnp.float32).astype(jnp.bfloat16)


class Plan:
    def __init__(self, rows, cols, shape):
        self.rows, self.cols = rows, cols
        self.rt = shape[0] // TILE
        self.ht = shape[1] // TILE
        self.tiles = self.rt * rows
        self.z = rows // Q
        self.pt = self.rt * Q
        self.slots = self.ht // Q
        at = 0
        for name, size in (
            ("lab", self.tiles),
            ("ordc", self.tiles),
            ("ordg", self.tiles),
            ("a0", 2 * NIRREP),
            ("m", 2 * NIRREP),
            ("s0", 2 * Q * NIRREP),
            ("u", 2 * Q * NIRREP),
            ("n", NIRREP),
            ("start", NIRREP),
            ("nz", self.z * NIRREP),
            ("zst", self.z * NIRREP),
        ):
            setattr(self, name, at)
            at += size
        self.table = at


def tables(plan, lab):
    t = plan.tiles
    index = jnp.arange(t, dtype=jnp.int32)
    half = index // plan.ht
    less = (lab[None, :] < lab[:, None]) | ((lab[None, :] == lab[:, None]) & (index[None, :] < index[:, None]))
    grank = jnp.sum(less, axis=1, dtype=jnp.int32)
    crank = jnp.sum(less & (half[None, :] == half[:, None]), axis=1, dtype=jnp.int32)
    ordg = jnp.sum(jnp.where(grank[None, :] == index[:, None], index[None, :], 0), axis=1)
    ordc = jnp.sum(jnp.where((crank + half * plan.ht)[None, :] == index[:, None], index[None, :], 0), axis=1)
    irreps = jnp.arange(NIRREP, dtype=jnp.int32)
    hot = lab[:, None] == irreps[None, :]
    below = lab[:, None] < irreps[None, :]

    def count(mask, which):
        return jnp.sum(mask[None] & which[:, :, None], axis=1, dtype=jnp.int32)

    in_half = half[None, :] == jnp.arange(2)[:, None]
    group = jnp.arange(2 * Q, dtype=jnp.int32)
    in_group = (half * Q + crank % Q)[None, :] == group[:, None]
    plane = index[None, :] // plan.pt == jnp.arange(plan.z)[:, None]
    before = index[None, :] // plan.pt < jnp.arange(plan.z)[:, None]
    row = index[None, :] // plan.rt == jnp.arange(plan.rows)[:, None]
    everything = jnp.ones((1, t), jnp.bool_)
    m = count(hot, in_half)
    u = count(hot, in_group)
    nz = count(hot, plane)
    nr = count(hot, row)
    table = jnp.concatenate(
        [
            lab,
            ordc,
            ordg,
            count(below, in_half).reshape(-1),
            m.reshape(-1),
            count(below, in_group).reshape(-1),
            u.reshape(-1),
            count(hot, everything).reshape(-1),
            count(below, everything).reshape(-1),
            nz.reshape(-1),
            count(hot, before).reshape(-1),
        ]
    )
    need = (
        jnp.max(jnp.sum(nr[:, None, :] * m[None], axis=2)),
        jnp.max(jnp.sum(nr[:, None, :] * u[None], axis=2)),
        jnp.max(jnp.sum(nz[:, None, :] * u[None], axis=2)),
    )
    return table, need


def place():
    r = lax.axis_index("row")
    return r, r // Q, r % Q, lax.axis_index("col")


def tile_of(ref, k, j):
    return ref.at[pl.ds(pl.multiple_of(k * TILE, TILE), TILE), pl.ds(pl.multiple_of(j * TILE, TILE), TILE)]


def drain(count, copy):
    lax.fori_loop(0, count, lambda _, c: (copy.wait(), c)[1], 0)


def pack_amplitudes(plan, tab, src, *rest):
    outs, sem = rest[:Q], rest[Q]
    r, z, q, c = place()
    total = 0
    for d in range(Q):
        g = (c * Q + (q ^ d)) * NIRREP

        def per_row(k, t):
            lab = tab[plan.lab + r * plan.rt + k]
            s0, u = tab[plan.s0 + g + lab], tab[plan.u + g + lab]

            def per_slot(s, t):
                j = tab[plan.ordc + c * plan.ht + (q ^ d) + Q * s] - c * plan.ht
                pltpu.make_async_copy(tile_of(src, k, j), outs[d].at[t], sem).start()
                return t + 1

            return lax.fori_loop(s0, s0 + u, per_slot, t)

        total = total + lax.fori_loop(0, plan.rt, per_row, 0)
    drain(total, pltpu.make_async_copy(tile_of(src, 0, 0), outs[0].at[0], sem))


def pack_integrals(plan, tab, src, low, high, sem):
    r, z, q, c = place()
    part = low.shape[0]

    def per_row(k, t):
        lab = tab[plan.lab + r * plan.rt + k]
        a0, m = tab[plan.a0 + c * NIRREP + lab], tab[plan.m + c * NIRREP + lab]

        def per_col(x, t):
            j = tab[plan.ordc + c * plan.ht + x] - c * plan.ht

            @pl.when(t < part)
            def _():
                pltpu.make_async_copy(tile_of(src, k, j), low.at[t], sem).start()

            @pl.when(t >= part)
            def _():
                pltpu.make_async_copy(tile_of(src, k, j), high.at[t - part], sem).start()

            return t + 1

        return lax.fori_loop(a0, a0 + m, per_col, t)

    total = lax.fori_loop(0, plan.rt, per_row, 0)
    drain(total, pltpu.make_async_copy(tile_of(src, 0, 0), low.at[0], sem))


def merge_lists(plan, tab, *rest):
    lists, out, sem = rest[:Q], rest[Q], rest[Q + 1]
    r, z, q, c = place()
    g = (c * Q + q) * NIRREP

    def held(p):
        return lax.fori_loop(
            0, plan.rt, lambda k, t: t + tab[plan.u + g + tab[plan.lab + (z * Q + p) * plan.rt + k]], 0
        )

    counts = [held(p) for p in range(Q)]
    for d in range(Q):
        p = q ^ d
        first = sum(jnp.where(other < p, counts[other], 0) for other in range(Q))
        size = sum(jnp.where(other == p, counts[other], 0) for other in range(Q))

        def one(t, carry):
            pltpu.make_async_copy(lists[d].at[t], out.at[first + t], sem).start()
            return carry

        lax.fori_loop(0, size, one, 0)
    drain(sum(counts), pltpu.make_async_copy(lists[0].at[0], out.at[0], sem))


def multiply(plan, va, cap, vp, tab, *rest):
    na, nb = 4 * Q, 2 * plan.z - 1
    a_in, b_in, outs = rest[:na], rest[na : na + nb], rest[na + nb : na + nb + Q]
    a_all, b_all, c_all, acc, off_a, off_b, off_c, sem_a, sem_b, sem_c = rest[na + nb + Q :]
    r, z, q, c = place()
    g = (c * Q + q) * NIRREP
    part = va // 2

    a_copies = []
    for d in range(Q):
        for h in range(2):
            for e in range(2):
                n = (d * 2 + h) * 2 + e
                a_copies.append(
                    pltpu.make_async_copy(a_in[n], a_all.at[pl.ds((d * 2 + h) * va + e * part, part)], sem_a.at[n])
                )

    def b_copy(n, unit):
        return pltpu.make_async_copy(b_in[n], b_all.at[pl.ds(unit * vp, vp)], sem_b.at[n])

    def each_unit(act):
        act(b_copy(0, z))
        for h in range(1, plan.z):

            @pl.when(z - h >= 0)
            def _():
                act(b_copy(2 * h - 1, z - h))

            @pl.when(z + h < plan.z)
            def _():
                act(b_copy(2 * h, z + h))

    for copy in a_copies:
        copy.start()
    each_unit(lambda copy: copy.start())

    zero_a, zero_b, spare = 2 * Q * va, plan.z * vp, Q * cap
    a_all[zero_a] = jnp.zeros((TILE, TILE), a_all.dtype)
    b_all[zero_b] = jnp.zeros((TILE, TILE), b_all.dtype)

    def plane_offsets(p, _):
        def one(k, run):
            off_b[p * plan.pt + k] = run
            return run + tab[plan.u + g + tab[plan.lab + p * plan.pt + k]]

        return lax.fori_loop(0, plan.pt, one, 0)

    lax.fori_loop(0, plan.z, plane_offsets, 0)

    def row_offsets(p, _):
        def one(k, run):
            i = p * plan.rt + k
            lab = tab[plan.lab + z * plan.pt + i]
            off_a[2 * i] = run[0]
            off_a[2 * i + 1] = run[1]
            off_c[i] = run[2]
            return (
                run[0] + tab[plan.m + lab],
                run[1] + tab[plan.m + NIRREP + lab],
                run[2] + tab[plan.u + g + lab],
            )

        lax.fori_loop(0, plan.rt, one, (0, 0, 0))
        return 0

    lax.fori_loop(0, Q, row_offsets, 0)

    for copy in a_copies:
        copy.wait()
    each_unit(lambda copy: copy.wait())

    def per_label(lab, carry):
        n, start = tab[plan.n + lab], tab[plan.start + lab]
        nz, zst = tab[plan.nz + z * NIRREP + lab], tab[plan.zst + z * NIRREP + lab]
        m0 = tab[plan.m + lab]
        u, s0 = tab[plan.u + g + lab], tab[plan.s0 + g + lab]

        def per_group(gi, carry):
            row = []
            for a in range(GRP):
                i = tab[plan.ordg + start + zst + jnp.minimum(gi * GRP + a, nz - 1)] - z * plan.pt
                row.append((i, (i // plan.rt) ^ q))

            def per_chunk(sc, carry):
                acc[...] = jnp.zeros_like(acc)

                def per_inner(kc, carry):
                    a_cols, b_rows = [], []
                    for b in range(GRP):
                        kk = kc * GRP + b
                        live = kk < n
                        inner = tab[plan.ordg + start + jnp.minimum(kk, n - 1)]
                        upper = (kk >= m0).astype(jnp.int32)
                        x = kk - upper * m0
                        tiles = []
                        for i, d in row:
                            at = (d * 2 + (upper ^ c)) * va + off_a[2 * i + upper] + x
                            tiles.append(a_all[jnp.where(live, at, zero_a)])
                        a_cols.append(jnp.concatenate(tiles, axis=0))
                        tiles = []
                        for w in range(2):
                            s = sc * 2 + w
                            at = (inner // plan.pt) * vp + off_b[inner] + s
                            tiles.append(b_all[jnp.where(live & (s < u), at, zero_b)])
                        b_rows.append(jnp.concatenate(tiles, axis=1))
                    acc[...] += jnp.dot(
                        jnp.concatenate(a_cols, axis=1),
                        jnp.concatenate(b_rows, axis=0),
                        preferred_element_type=jnp.float32,
                    )
                    return carry

                lax.fori_loop(0, pl.cdiv(n, GRP), per_inner, 0)
                for a, (i, d) in enumerate(row):
                    for w in range(2):
                        s = sc * 2 + w
                        at = jnp.where(s < u, d * cap + off_c[i] + s, spare)
                        c_all[at] = acc[a * TILE : (a + 1) * TILE, w * TILE : (w + 1) * TILE].astype(c_all.dtype)
                return carry

            return lax.fori_loop(0, pl.cdiv(u, 2), per_chunk, carry)

        return lax.fori_loop(0, pl.cdiv(nz, GRP), per_group, carry)

    lax.fori_loop(0, NIRREP, per_label, 0)
    out_copies = [pltpu.make_async_copy(c_all.at[pl.ds(d * cap, cap)], outs[d], sem_c.at[d]) for d in range(Q)]
    for copy in out_copies:
        copy.start()
    for copy in out_copies:
        copy.wait()


def unpack(plan, tab, *rest):
    lists, out, sem = rest[:Q], rest[Q], rest[Q + 1]
    r, z, q, c = place()

    def clear(k, carry):
        out[pl.ds(pl.multiple_of(k * 16, 16), 16), :] = jnp.zeros((16, out.shape[1]), out.dtype)
        return carry

    lax.fori_loop(0, out.shape[0] // 16, clear, 0)
    total = 0
    for d in range(Q):
        g = (c * Q + (q ^ d)) * NIRREP

        def per_row(k, t):
            lab = tab[plan.lab + r * plan.rt + k]
            s0, u = tab[plan.s0 + g + lab], tab[plan.u + g + lab]

            def per_slot(s, t):
                j = tab[plan.ordc + c * plan.ht + (q ^ d) + Q * s] - c * plan.ht
                pltpu.make_async_copy(lists[d].at[t], tile_of(out, k, j), sem).start()
                return t + 1

            return lax.fori_loop(s0, s0 + u, per_slot, t)

        total = total + lax.fori_loop(0, plan.rt, per_row, 0)
    drain(total, pltpu.make_async_copy(lists[0].at[0], tile_of(out, 0, 0), sem))


ANY = pl.BlockSpec(memory_space=pl.ANY)
WHOLE = pl.BlockSpec(memory_space=pltpu.VMEM)


def call(body, name, tab, args, outs, out_spec, scratch, cost):
    return pl.pallas_call(
        body,
        name=name,
        out_shape=outs,
        grid_spec=pltpu.PrefetchScalarGridSpec(
            num_scalar_prefetch=1,
            grid=(),
            in_specs=[ANY] * len(args),
            out_specs=jax.tree.map(lambda _: out_spec, outs),
            scratch_shapes=scratch,
        ),
        compiler_params=pltpu.CompilerParams(vmem_limit_bytes=60 * 1024 * 1024),
        cost_estimate=pl.CostEstimate(flops=cost[0], bytes_accessed=cost[1], transcendentals=0),
    )(tab, *args)


def blocked(plan, sizes, integrals, amplitudes, tab):
    va, cap, vp = sizes
    dtype = integrals.dtype

    def tiles(n):
        return jax.ShapeDtypeStruct((n, TILE, TILE), dtype)

    dma = pltpu.SemaphoreType.DMA
    nbytes = TILE * TILE * dtype.itemsize

    def across(x, d):
        return lax.ppermute(x, "row", [(i, i ^ d) for i in range(plan.rows)])

    def along(x, step, hop):
        pairs = []
        for i in range(plan.rows):
            p = i // Q
            if 0 <= p + step < plan.z and 0 <= p - (hop - 1) * step < plan.z:
                pairs.append((i, i + step * Q))
        return lax.ppermute(x, "row", pairs)

    def swap(x):
        return lax.ppermute(x, "col", [(0, 1), (1, 0)])

    sent = call(
        functools.partial(pack_amplitudes, plan), "pack_amplitudes", tab, [amplitudes],
        [tiles(cap)] * Q, WHOLE, [dma(())], (0, 2 * Q * cap * nbytes),
    )
    got = [sent[0]] + [across(sent[d], d) for d in range(1, Q)]
    low, high = call(
        functools.partial(pack_integrals, plan), "pack_integrals", tab, [integrals],
        [tiles(va // 2)] * 2, WHOLE, [dma(())], (0, 2 * va * nbytes),
    )
    unit = call(
        functools.partial(merge_lists, plan), "merge_lists", tab, got,
        tiles(vp), WHOLE, [dma(())], (0, 2 * vp * nbytes),
    )
    low, high, unit = lax.optimization_barrier((low, high, unit))
    units, right, left = [unit], unit, unit
    for hop in range(1, plan.z):
        right, left = along(right, 1, hop), along(left, -1, hop)
        units += [right, left]

    low_1, high_1, low_2, high_2 = across(low, 1), across(high, 1), across(low, 2), across(high, 2)
    parts = [low, high, low_1, high_1, low_2, high_2, across(low_1, 2), across(high_2, 1)]
    a_lists = []
    for d in range(Q):
        mine = parts[2 * d : 2 * d + 2]
        a_lists += mine + [swap(x) for x in mine]

    product = call(
        functools.partial(multiply, plan, va, cap, vp), "multiply", tab, a_lists + units,
        [tiles(cap)] * Q, ANY,
        [
            pltpu.VMEM((2 * Q * va + 1, TILE, TILE), dtype),
            pltpu.VMEM((plan.z * vp + 1, TILE, TILE), dtype),
            pltpu.VMEM((Q * cap + 1, TILE, TILE), dtype),
            pltpu.VMEM((GRP * TILE, 2 * TILE), jnp.float32),
            pltpu.SMEM((2 * plan.pt,), jnp.int32),
            pltpu.SMEM((plan.tiles,), jnp.int32),
            pltpu.SMEM((plan.pt,), jnp.int32),
            dma((4 * Q,)),
            dma((2 * plan.z - 1,)),
            dma((Q,)),
        ],
        (2 * vp * plan.tiles * TILE**3 // 2, (2 * Q * va + plan.z * vp) * nbytes),
    )
    back = [product[0]] + [across(product[d], d) for d in range(1, Q)]
    return call(
        functools.partial(unpack, plan), "unpack", tab, back,
        jax.ShapeDtypeStruct(integrals.shape, dtype), WHOLE, [dma(())],
        (0, 2 * integrals.size * dtype.itemsize),
    )


def solution(mesh):
    rows, cols = mesh.shape["row"], mesh.shape["col"]

    def local(integrals, amplitudes, pair_irrep, tile_map):
        plan = Plan(rows, cols, integrals.shape)
        full = (plan.rt * plan.ht, plan.rt * plan.slots, plan.pt * plan.slots)
        if cols != 2 or rows % Q or plan.ht % Q or plan.tiles != cols * plan.ht or full != (128, 32, 128):
            return dense(integrals, amplitudes, pair_irrep, tile_map)
        table, need = tables(plan, tile_labels(pair_irrep, tile_map))
        sizes = CLASSES + (full,)
        fits = [sum((need[i] > size[i]).astype(jnp.int32) for i in range(3)) > 0 for size in sizes[:-1]]
        pick = sum(f.astype(jnp.int32) for f in fits)
        return lax.switch(
            pick,
            [functools.partial(blocked, plan, size) for size in sizes],
            integrals, amplitudes, table,
        )

    return jax.shard_map(
        local,
        mesh=mesh,
        in_specs=(P("row", "col"), P("row", "col"), P(), P()),
        out_specs=P("row", "col"),
        check_vma=False,
    )
```
